32 devices in a mesh: dp: 8 (over y, x, core), mp: 4 (over z).
Axes of the slice: x: 2, y: 2, z: 4, core: 2. Of those that a mesh axis runs over, the one named last changes fastest.
Arguments:
- latent: bfloat16 [8192, 1152], P('dp'), may hold values from -6 to 6
- condition: bfloat16 [8, 1152], P('dp'), may hold values from -6 to 6
- lengths: int32 [8], P('dp'), may hold values from 128 to 1024, as said below
- w_ada: bfloat16 [1152, 6912], P(None, 'mp'), may hold values from -0.1875 to 0.1875
- b_ada: bfloat16 [6912], P('mp'), may hold values from -3 to 3
- w_qkv: bfloat16 [1152, 3, 1152], P(None, None, 'mp'), may hold values from -0.1875 to 0.1875
- b_qv: bfloat16 [2, 1152], P(None, 'mp'), may hold values from -3 to 3
- w_out: bfloat16 [1152, 1152], P('mp'), may hold values from -0.75 to 0.75
- b_out: bfloat16 [1152], replicated, may hold values from -2 to 2
- w_fc1: bfloat16 [1152, 4608], P(None, 'mp'), may hold values from -0.1875 to 0.1875
- b_fc1: bfloat16 [4608], P('mp'), may hold values from -2 to 2
- w_fc2: bfloat16 [4608, 1152], P('mp'), may hold values from -0.09375 to 0.09375
- b_fc2: bfloat16 [1152], replicated, may hold values from -2 to 2
- cotangent: bfloat16 [8192, 1152], P('dp'), may hold values from -6 to 6
Outputs:
- output: bfloat16 [8192, 1152], P('dp')
- grad_latent: bfloat16 [8192, 1152], P('dp')
- grad_condition: float32 [8, 1152], P('dp')
- grad_w_ada: float32 [1152, 6912], P(None, 'mp')
- grad_b_ada: float32 [6912], P('mp')
- grad_w_qkv: float32 [1152, 3, 1152], P(None, None, 'mp')
- grad_b_qv: float32 [2, 1152], P(None, 'mp')
- grad_w_out: float32 [1152, 1152], P('mp')
- grad_b_out: float32 [1152], replicated
- grad_w_fc1: float32 [1152, 4608], P(None, 'mp')
- grad_b_fc1: float32 [4608], P('mp')
- grad_w_fc2: float32 [4608, 1152], P('mp')
- grad_b_fc2: float32 [1152], replicated
The draws below stay inside these ranges and needn't reach their ends.
Inputs may be any that keep to these rules, and one draw needn't show every extreme that they name: The first lengths[s] of sample s's 1024 rows are real tokens, the rest padding; some sample has all 1024 rows real.
All inputs are finite; a program needn't handle non-finite values.
Results may differ from the reference program's by a relative error of at most 0.02.
The reference program's roundings to bfloat16 on the way count: a program that leaves them out, or rounds other values in their place, can miss the bound.
Values may be sent and summed in bfloat16 or wider, within the bound.
No kernel may reach another device: no remote copies, remote signals or barrier semaphores. Data moves between devices by JAX's collectives and lax.ppermute only.
A program may use at most 192 MiB of HBM per device.

```python
import math
import jax
import jax.numpy as jnp
from jax import lax

D = 1152
HD = 72
FF = 4608
SEQ = 1024
SAMPLES = 8
N_MP = 4


def draw_lengths(key, part):
    first, second = jax.random.split(key)
    counts = jax.random.randint(first, (SAMPLES,), SEQ // 8, SEQ + 1, dtype=jnp.int32)
    chosen = jax.random.randint(second, (), 0, SAMPLES, dtype=jnp.int32)
    return jnp.where(jnp.arange(SAMPLES, dtype=jnp.int32) == chosen, SEQ, counts).astype(jnp.int32)


def levels(own_key, shape, pieces, smallest, top_value):
    factor_of, own = 1.0, jax.random.fold_in(own_key, 6)
    for dim, blocks in pieces:
        heights = jnp.exp(jax.random.uniform(jax.random.fold_in(own, dim), (blocks,), jnp.float32, smallest / len(pieces), top_value / len(pieces)))
        factor_of = factor_of * jnp.repeat(heights, shape[dim] // blocks).reshape([-1 if axis == dim else 1 for axis in range(len(shape))])
    return factor_of


def bell_draw(own_key, shape, width, bound, cuts=(), kind=jnp.bfloat16):
    array = jax.random.normal(own_key, shape, jnp.float32) * width
    if len(cuts) > 0:
        array = levels(own_key, shape, cuts, -0.22, 0.18) * array
    return jnp.clip(array, min=-bound, max=bound).astype(kind)


def setup_inputs(seed: int = 0) -> dict:
    arg_keys = jax.random.split(jax.random.key(seed), 15)
    latent = bell_draw(arg_keys[0], (SAMPLES * SEQ, D), 1.0, 6.0, ((0, 8),))
    condition = bell_draw(arg_keys[1], (SAMPLES, D), 1.0, 6.0, ((0, 8),))
    lengths = draw_lengths(jax.random.fold_in(arg_keys[14], 71), 0)
    w_ada = bell_draw(arg_keys[3], (D, 6 * D), D ** -0.5, 0.1875, ((1, 4),))
    b_ada = bell_draw(arg_keys[4], (6 * D,), 0.5, 3.0, ((0, 4),))
    w_qkv = bell_draw(arg_keys[5], (D, 3, D), D ** -0.5, 0.1875, ((2, 4),))
    b_qv = bell_draw(arg_keys[6], (2, D), 0.5, 3.0, ((1, 4),))
    w_out = bell_draw(arg_keys[7], (D, D), (D // 16) ** -0.5, 0.75, ((0, 4),))
    b_out = bell_draw(arg_keys[8], (D,), 0.3, 2.0)
    w_fc1 = bell_draw(arg_keys[9], (D, FF), D ** -0.5, 0.1875, ((1, 4),))
    b_fc1 = bell_draw(arg_keys[10], (FF,), 0.3, 2.0, ((0, 4),))
    w_fc2 = bell_draw(arg_keys[11], (FF, D), FF ** -0.5, 0.09375, ((0, 4),))
    b_fc2 = bell_draw(arg_keys[12], (D,), 0.3, 2.0)
    cotangent = bell_draw(arg_keys[13], (SAMPLES * SEQ, D), 1.0, 6.0, ((0, 8),))
    return dict(latent=latent, condition=condition, lengths=lengths, w_ada=w_ada, b_ada=b_ada, w_qkv=w_qkv, b_qv=b_qv, w_out=w_out, b_out=b_out, w_fc1=w_fc1, b_fc1=b_fc1, w_fc2=w_fc2, b_fc2=b_fc2, cotangent=cotangent)


PRECISE = lax.Precision.HIGHEST
EPSILON = 1e-06

@jax.custom_vjp
def low(v):
    return lax.optimization_barrier(v.astype(jnp.bfloat16)).astype(jnp.float32)

@jax.custom_vjp
def low_back(v):
    return v

def low_keep(v):
    return (low(v), None)

def low_pass(kept, grad):
    return (grad,)

def back_keep(v):
    return (v, None)

def back_low(kept, grad):
    return (low(grad),)
low.defvjp(low_keep, low_pass)
low_back.defvjp(back_keep, back_low)

def layer_norm(values):
    row_mean = lax.optimization_barrier(jnp.mean(values, axis=-1, keepdims=True))
    centred = values - row_mean
    row_var = lax.optimization_barrier(jnp.mean(centred * centred, axis=-1, keepdims=True))
    return centred * lax.rsqrt(row_var + EPSILON)

def modulate(values, scale_tok, shift_tok):
    return layer_norm(values) * (1.0 + scale_tok) + shift_tok

def gelu_tanh(values):
    return jax.nn.gelu(values, approximate=True)

def attend_sample(packed):
    query_rows, key_rows, value_rows, real_count = packed
    head_count = query_rows.shape[1] // HD
    query_heads = query_rows.reshape(SEQ, head_count, HD)
    key_heads = key_rows.reshape(SEQ, head_count, HD)
    value_heads = value_rows.reshape(SEQ, head_count, HD)
    scores = jnp.einsum('qhd,khd->hqk', query_heads, key_heads, precision=PRECISE) * (1.0 / math.sqrt(HD))
    scores = low_back(scores)
    is_valid = jnp.arange(SEQ, dtype=jnp.int32) < real_count
    scores = jnp.where(is_valid[None, None, :], scores, -1e+30)
    probability = low(jax.nn.softmax(scores, axis=-1))
    mixed = jnp.einsum('hqk,khd->qhd', probability, value_heads, precision=PRECISE)
    return mixed.reshape(SEQ, head_count * HD)

def block_forward(params, block_latent, block_cond, block_len):
    w_ada, b_ada, w_qkv, b_qv, w_out, b_out, w_fc1, b_fc1, w_fc2, b_fc2 = params
    sample_count = block_cond.shape[0]
    all_rows = sample_count * SEQ
    silu_cond = jax.nn.silu(block_cond)
    modulation = (jnp.dot(silu_cond, w_ada, precision=PRECISE) + b_ada).reshape(sample_count, 6, 1, D)
    inputs = block_latent.reshape(sample_count, SEQ, D)
    normed_a = low(modulate(inputs, modulation[:, 1], modulation[:, 0])).reshape(all_rows, D)
    group_width = D // N_MP
    group_hidden = FF // N_MP
    attn_sum = jnp.zeros((all_rows, D), jnp.float32)
    for group in range(N_MP):
        group_in = low_back(normed_a)
        columns = slice(group * group_width, (group + 1) * group_width)
        query = low_back(low(jnp.dot(group_in, w_qkv[:, 0, columns], precision=PRECISE) + b_qv[0, columns]))
        key_rows = low_back(low(jnp.dot(group_in, w_qkv[:, 1, columns], precision=PRECISE)))
        value_rows = low_back(low(jnp.dot(group_in, w_qkv[:, 2, columns], precision=PRECISE) + b_qv[1, columns]))
        mixed = lax.map(jax.checkpoint(attend_sample), (query.reshape(sample_count, SEQ, group_width), key_rows.reshape(sample_count, SEQ, group_width), value_rows.reshape(sample_count, SEQ, group_width), block_len))
        attended = low_back(low(mixed.reshape(all_rows, group_width)))
        attn_sum = attn_sum + low(jnp.dot(attended, w_out[columns], precision=PRECISE))
    attn_branch = low_back(attn_sum + b_out)
    middle = inputs + modulation[:, 2] * attn_branch.reshape(sample_count, SEQ, D)
    normed_m = low(modulate(middle, modulation[:, 4], modulation[:, 3])).reshape(all_rows, D)
    mlp_sum = jnp.zeros((all_rows, D), jnp.float32)
    for group in range(N_MP):
        group_in = low_back(normed_m)
        columns = slice(group * group_hidden, (group + 1) * group_hidden)
        hidden_pre = low_back(jnp.dot(group_in, w_fc1[:, columns], precision=PRECISE) + b_fc1[columns])
        activated = low(gelu_tanh(hidden_pre))
        mlp_sum = mlp_sum + low(jnp.dot(activated, w_fc2[columns], precision=PRECISE))
    mlp_branch = low_back(mlp_sum + b_fc2)
    result = middle + modulation[:, 5] * mlp_branch.reshape(sample_count, SEQ, D)
    return result.reshape(all_rows, D)

def reference(latent, condition, lengths, w_ada, b_ada, w_qkv, b_qv, w_out, b_out, w_fc1, b_fc1, w_fc2, b_fc2, cotangent):
    params = (w_ada.astype(jnp.float32), b_ada.astype(jnp.float32), w_qkv.astype(jnp.float32), b_qv.astype(jnp.float32), w_out.astype(jnp.float32), b_out.astype(jnp.float32), w_fc1.astype(jnp.float32), b_fc1.astype(jnp.float32), w_fc2.astype(jnp.float32), b_fc2.astype(jnp.float32))
    per_block = 4 if SAMPLES % 4 == 0 else 1
    block_count = SAMPLES // per_block
    latents = latent.astype(jnp.float32).reshape(block_count, per_block * SEQ, D)
    conds = condition.astype(jnp.float32).reshape(block_count, per_block, D)
    counts = lengths.reshape(block_count, per_block)
    cotans = cotangent.astype(jnp.float32).reshape(block_count, per_block * SEQ, D)

    def block_step(running, block_data):
        block_latent, block_cond, block_len, block_cot = block_data

        def forward_here(weights, latent_in, cond_in):
            return block_forward(weights, latent_in, cond_in, block_len)
        block_out, pullback = jax.vjp(forward_here, params, block_latent, block_cond)
        grad_params, grad_in, grad_cond = pullback(block_cot)
        running = jax.tree.map(jnp.add, running, grad_params)
        return (running, (block_out.astype(jnp.bfloat16), grad_in.astype(jnp.bfloat16), grad_cond))
    start_sums = jax.tree.map(jnp.zeros_like, params)
    sums, (outputs, grad_inputs, grad_conds) = lax.scan(block_step, start_sums, (latents, conds, counts, cotans))
    return (outputs.reshape(SAMPLES * SEQ, D), grad_inputs.reshape(SAMPLES * SEQ, D), grad_conds.reshape(SAMPLES, D), sums[0], sums[1], sums[2], sums[3], sums[4], sums[5], sums[6], sums[7], sums[8], sums[9])
```

```python
import math

import jax
import jax.numpy as jnp
from jax import lax
from jax.experimental import pallas as pl
from jax.experimental.pallas import tpu as pltpu
from jax.sharding import PartitionSpec as P

HD = 72
HP = 128
EPSILON = 1e-06
F32 = jnp.float32
BF16 = jnp.bfloat16
PRECISE = lax.Precision.HIGHEST
LOG2E = math.log2(math.e)
SCORE = LOG2E / math.sqrt(HD)
SCALING = 1.0 / math.sqrt(HD)
MIB = 1 << 20
NT = (((1,), (1,)), ((), ()))
TN = (((0,), (0,)), ((), ()))
IN_HOP = ((0, 1), (3, 2))
MID_HOP = ((1, 2), (2, 1))
OUT_HOP = ((1, 0), (2, 3))
SHIFT_A, SCALE_A, GATE_A, SHIFT_M, SCALE_M, GATE_M = range(6)


def dot(a, b):
    return jnp.dot(a, b, preferred_element_type=F32)


def dot_nt(a, b):
    return lax.dot_general(a, b, NT, preferred_element_type=F32)


def dot_tn(a, b):
    return lax.dot_general(a, b, TN, preferred_element_type=F32)


def params(mib):
    return pltpu.CompilerParams(vmem_limit_bytes=mib * MIB)


def cost(flops, size):
    return pl.CostEstimate(flops=int(flops), bytes_accessed=int(size), transcendentals=0)


def normalize(values):
    row_mean = jnp.mean(values, axis=-1, keepdims=True)
    centred = values - row_mean
    inverse = lax.rsqrt(jnp.mean(centred * centred, axis=-1, keepdims=True) + EPSILON)
    return centred * inverse, inverse


def normalize_back(normal, inverse, grad):
    mean_grad = jnp.mean(grad, axis=-1, keepdims=True)
    mean_both = jnp.mean(grad * normal, axis=-1, keepdims=True)
    return inverse * (grad - mean_grad - normal * mean_both)


def total(values):
    return jnp.sum(values, axis=0, keepdims=True)


def full(shape, dtype):
    return jax.ShapeDtypeStruct(shape, dtype)


def call(kernel, index, inputs, outputs, scalars=(), name=None, mib=32, flops=0, size=0):
    operands, in_specs, out_specs, shapes, aliases = [], [], [], [], {}

    def spec(shape, rows):
        if rows is None:
            return pl.BlockSpec(shape, lambda i, *_: (0,) * len(shape))
        if rows == "lanes":
            return pl.BlockSpec((shape[0], BLOCK_LANES), lambda i, *_: (0, index))
        return pl.BlockSpec((rows, *shape[1:]), lambda i, *_: (index, 0))

    for value, rows in inputs:
        operands.append(value)
        in_specs.append(spec(value.shape, rows))
    count = len(operands)
    for place, (shape, rows, buffer) in enumerate(outputs):
        shapes.append(shape)
        out_specs.append(spec(shape.shape, rows))
        if buffer is not None:
            aliases[len(scalars) + len(operands)] = place
            operands.append(buffer)
            in_specs.append(pl.BlockSpec(memory_space=pl.ANY))
    held = len(operands) - count

    def body(*refs):
        refs = list(refs)
        del refs[len(scalars) + count : len(scalars) + count + held]
        kernel(*refs)

    return pl.pallas_call(
        body,
        out_shape=shapes,
        grid_spec=pltpu.PrefetchScalarGridSpec(
            num_scalar_prefetch=len(scalars), grid=(1,), in_specs=in_specs, out_specs=out_specs
        ),
        input_output_aliases=aliases,
        compiler_params=params(mib),
        cost_estimate=cost(flops, size),
        name=name,
    )(*scalars, *operands)


BLOCK_LANES = 256


def thirds(values):
    high = values.astype(BF16).astype(F32)
    rest = values - high
    middle = rest.astype(BF16).astype(F32)
    return high, middle, rest - middle


def modulate_kernel(cond_ref, w_ref, b_ref, out_ref):
    step = pl.program_id(0)
    cond = cond_ref[...].astype(F32)
    rows = jnp.concatenate([*thirds(cond / (1.0 + jnp.exp(-cond))), jnp.zeros((5, cond.shape[1]), F32)])
    part = total(dot(rows.astype(BF16), w_ref[...]))

    @pl.when(step == 0)
    def _():
        out_ref[...] = b_ref[...].astype(F32) + part

    @pl.when(step > 0)
    def _():
        out_ref[...] += part


def modulate(condition, weight, bias):
    model, wide = weight.shape
    step = 384
    return pl.pallas_call(
        modulate_kernel,
        out_shape=full((1, wide), F32),
        grid=(model // step,),
        in_specs=[
            pl.BlockSpec((1, step), lambda i: (0, i)),
            pl.BlockSpec((step, wide), lambda i: (i, 0)),
            pl.BlockSpec((1, wide), lambda i: (0, 0)),
        ],
        out_specs=pl.BlockSpec((1, wide), lambda i: (0, 0)),
        compiler_params=params(16),
        cost_estimate=cost(16 * model * wide, 2 * model * wide),
        name="modulate",
    )(condition, weight, bias.reshape(1, wide))


def condition_kernel(grad_ref, w_ref, out_ref):
    grad = grad_ref[...]
    rows = jnp.concatenate([*thirds(grad), jnp.zeros((5, grad.shape[1]), F32)])
    out_ref[...] = total(dot_nt(rows.astype(BF16), w_ref[...]))


def condition_term(grad, weight):
    model, wide = weight.shape
    step = 384
    return pl.pallas_call(
        condition_kernel,
        out_shape=full((1, model), F32),
        grid=(model // step,),
        in_specs=[
            pl.BlockSpec((1, wide), lambda i: (0, 0)),
            pl.BlockSpec((step, wide), lambda i: (i, 0)),
        ],
        out_specs=pl.BlockSpec((1, step), lambda i: (0, i)),
        compiler_params=params(16),
        cost_estimate=cost(16 * model * wide, 2 * model * wide),
        name="condition_term",
    )(grad, weight)


def outer_kernel(a_ref, b_ref, out_ref):
    a, b = thirds(a_ref[...]), thirds(b_ref[...])
    left = jnp.concatenate([a[0], a[0], a[1], a[0], a[1], a[2]]).astype(BF16)
    right = jnp.concatenate([b[0], b[1], b[0], b[2], b[1], b[0]]).astype(BF16)
    out_ref[...] = dot_tn(left, right)


def outer(a, b):
    samples, model = a.shape
    wide = b.shape[1]
    step = 384
    return pl.pallas_call(
        outer_kernel,
        out_shape=full((model, wide), F32),
        grid=(model // step,),
        in_specs=[
            pl.BlockSpec((samples, step), lambda i: (0, i)),
            pl.BlockSpec((samples, wide), lambda i: (0, 0)),
        ],
        out_specs=pl.BlockSpec((step, wide), lambda i: (i, 0)),
        compiler_params=params(24),
        cost_estimate=cost(12 * samples * model * wide, 4 * model * wide),
        name="outer",
    )(a, b)


def spread(ref, values, heads, extra=None):
    ref[...] = jnp.zeros_like(ref)
    for head in range(heads):
        ref[:, head * HP : head * HP + HD] = values[:, head * HD : (head + 1) * HD].astype(BF16)
        if extra is not None:
            ref[:, head * HP + HD : head * HP + HD + 1] = extra


def project_kernel(len_ref, lat_ref, mod_ref, w_ref, b_ref, n_ref, q_ref, k_ref, v_ref):
    rows, width = q_ref.shape
    heads = width // HP
    group = heads * HD
    first = pl.program_id(0) * rows
    normal, _ = normalize(lat_ref[...].astype(F32))
    scale = 1.0 + mod_ref[SCALE_A : SCALE_A + 1, :]
    normed = (normal * scale + mod_ref[SHIFT_A : SHIFT_A + 1, :]).astype(BF16)
    n_ref[...] = normed
    found = dot(normed, w_ref[...]) + b_ref[...]
    ones = jnp.ones((rows, 1), BF16)
    row = lax.broadcasted_iota(jnp.int32, (rows, 1), 0) + first
    hidden = jnp.where(row >= len_ref[0], -1e30, 0.0).astype(BF16)
    spread(q_ref, found[:, :group], heads, ones)
    spread(k_ref, found[:, group : 2 * group], heads, hidden)
    spread(v_ref, found[:, 2 * group :], heads, ones)


def project(lengths, latent, mod, weight, bias, block):
    tokens, model = latent.shape
    width = weight.shape[1] // 3 // HD * HP
    rows = lambda i, *_: (i, 0)
    whole = lambda i, *_: (0, 0)
    return pl.pallas_call(
        project_kernel,
        out_shape=[full((tokens, model), BF16)] + [full((tokens, width), BF16)] * 3,
        grid_spec=pltpu.PrefetchScalarGridSpec(
            num_scalar_prefetch=1,
            grid=(tokens // block,),
            in_specs=[
                pl.BlockSpec((block, model), rows),
                pl.BlockSpec(mod.shape, whole),
                pl.BlockSpec(weight.shape, whole),
                pl.BlockSpec(bias.shape, whole),
            ],
            out_specs=[pl.BlockSpec((block, model), rows)]
            + [pl.BlockSpec((block, width), rows)] * 3,
        ),
        compiler_params=params(32),
        cost_estimate=cost(6 * tokens * model * width, tokens * model * 8),
        name="project",
    )(lengths, latent, mod, weight, bias)


def attend_kernel(q_ref, k_ref, v_ref, wo_ref, term_ref, att_ref, mix_ref, lse_ref):
    rows, width = q_ref.shape
    lane = lax.broadcasted_iota(jnp.int32, (rows, HP), 1)
    stats = jnp.zeros((rows, HP), F32)
    for head in range(width // HP):
        at = slice(head * HP, (head + 1) * HP)
        scores = dot_nt(q_ref[:, at], k_ref[:, at])
        top = jnp.max(scores, axis=-1, keepdims=True)
        weights = jnp.exp2((scores - top) * SCORE).astype(BF16)
        mixed = dot(weights, v_ref[:, at])
        row_total = mixed[:, HD : HD + 1]
        mixed = mixed / row_total
        mix_ref[:, at] = mixed
        att_ref[:, head * HD : (head + 1) * HD] = mixed[:, :HD].astype(BF16)
        stats = jnp.where(lane == head, top * SCORE + jnp.log2(row_total), stats)
    lse_ref[...] = stats.T[: lse_ref.shape[0], :]
    term_ref[...] = dot(att_ref[...], wo_ref[...]).astype(BF16)


def attend(query, key, value, w_out, held, index, block):
    tokens, width = query.shape
    group, model = w_out.shape
    return call(
        attend_kernel, index,
        [(query, block), (key, None), (value, None), (w_out, None)],
        [
            (full((block, model), BF16), None, None),
            (full((tokens, group), BF16), block, held[0]),
            (full((tokens, width), F32), block, held[1]),
            (full((8, tokens), F32), "lanes", held[2]),
        ],
        name="attend", flops=4 * block * tokens * width, size=6 * tokens * width,
    )


def feed_kernel(
    end_ref, near_ref, far_ref, lat_ref, cot_ref, mod_ref, bo_ref, w1_ref, b1_ref, w2_ref,
    term_ref, sum_ref, tot_ref, n_ref, act_ref, gh_ref, gm_ref,
):
    summed = jnp.where(end_ref[0] == 1, far_ref[...].astype(F32), near_ref[...].astype(F32))
    tot_ref[...] = summed.astype(BF16)
    branch = summed + bo_ref[...]
    middle = lat_ref[...].astype(F32) + mod_ref[GATE_A : GATE_A + 1, :] * branch
    normal, _ = normalize(middle)
    scale = 1.0 + mod_ref[SCALE_M : SCALE_M + 1, :]
    normed = (normal * scale + mod_ref[SHIFT_M : SHIFT_M + 1, :]).astype(BF16)
    n_ref[...] = normed
    grad_mlp = (mod_ref[GATE_M : GATE_M + 1, :] * cot_ref[...].astype(F32)).astype(BF16)
    gm_ref[...] = grad_mlp
    hidden = dot(normed, w1_ref[...]) + b1_ref[...]
    grad_act = dot_nt(grad_mlp, w2_ref[...])
    root = math.sqrt(2.0 / math.pi)
    square = hidden * hidden
    bend = jnp.tanh(root * hidden * (1.0 + 0.044715 * square))
    half = 0.5 * (1.0 + bend)
    act_ref[...] = (hidden * half).astype(BF16)
    slope = half + 0.5 * hidden * (1.0 - bend * bend) * (root * (1.0 + 3 * 0.044715 * square))
    grad_hidden = (slope * grad_act).astype(BF16)
    gh_ref[...] = grad_hidden
    sum_ref[0:1, :] = total(grad_hidden.astype(F32))
    term_ref[...] = dot_nt(grad_hidden, w1_ref[...]).astype(BF16)


def feed(end, near, far, latent, cotangent, mod, b_out, w_fc1, b_fc1, w_fc2, held, index, block):
    model, hidden = w_fc1.shape
    tokens = latent.shape[0]
    return call(
        feed_kernel, index,
        [
            (near, None), (far, None), (latent, block), (cotangent, block), (mod, None),
            (b_out, None), (w_fc1, None), (b_fc1, None), (w_fc2, None),
        ],
        [
            (full((block, model), BF16), None, None),
            (full((8, hidden), F32), None, None),
            (full((tokens, model), BF16), block, held[0]),
            (full((tokens, model), BF16), block, held[1]),
            (full((tokens, hidden), BF16), block, held[2]),
            (full((tokens, hidden), BF16), block, held[3]),
            (full((tokens, model), BF16), block, held[4]),
        ],
        scalars=(end,), name="feed", mib=40,
        flops=6 * block * model * hidden, size=4 * model * hidden + 12 * block * model,
    )


def middle_kernel(
    end_ref, near_ref, far_ref, tot_ref, lat_ref, cot_ref, mod_ref, bo_ref, wo_ref,
    sum_ref, ga_ref, gmid_ref, datt_ref,
):
    grad = jnp.where(end_ref[0] == 1, far_ref[...].astype(F32), near_ref[...].astype(F32))
    branch = tot_ref[...].astype(F32) + bo_ref[...]
    gate = mod_ref[GATE_A : GATE_A + 1, :]
    normal, inverse = normalize(lat_ref[...].astype(F32) + gate * branch)
    sum_ref[0:1, :] = total(grad)
    sum_ref[1:2, :] = total(grad * normal)
    scale = 1.0 + mod_ref[SCALE_M : SCALE_M + 1, :]
    grad_middle = cot_ref[...].astype(F32) + normalize_back(normal, inverse, grad * scale)
    gmid_ref[...] = grad_middle
    sum_ref[2:3, :] = total(grad_middle * branch)
    grad_attn = (gate * grad_middle).astype(BF16)
    ga_ref[...] = grad_attn
    sum_ref[3:4, :] = total(grad_attn.astype(F32))
    spread(datt_ref, dot_nt(grad_attn, wo_ref[...]), datt_ref.shape[1] // HP)


def middle_back(end, near, far, tot, latent, cotangent, mod, b_out, w_out, held, index, block):
    group, model = w_out.shape
    width = group // HD * HP
    tokens = latent.shape[0]
    return call(
        middle_kernel, index,
        [
            (near, None), (far, None), (tot, block), (latent, block), (cotangent, block),
            (mod, None), (b_out, None), (w_out, None),
        ],
        [
            (full((8, model), F32), None, None),
            (full((tokens, model), BF16), block, held[0]),
            (full((tokens, model), F32), block, held[1]),
            (full((tokens, width), BF16), block, held[2]),
        ],
        scalars=(end,), name="middle", flops=2 * block * model * width, size=16 * block * model,
    )


def attend_back_kernel(q_ref, k_ref, v_ref, do_ref, mix_ref, lse_ref, dq_ref, dk_ref, dv_ref, sk, sv, *, first):
    head = pl.program_id(0) + first
    tokens = q_ref.shape[0]
    block = 256
    key, value = k_ref[...], v_ref[...]

    def step(i, carry):
        at = pl.ds(pl.multiple_of(i * block, block), block)
        query, grad = q_ref[at, :], do_ref[at, :]
        both = grad.astype(F32) * mix_ref[at, :]
        inner = jnp.sum(both.T, axis=0, keepdims=True)
        prob = jnp.exp2(dot_nt(key, query) * SCORE - lse_ref[pl.ds(head, 1), at])
        grad_score = (prob * (dot_nt(value, grad) - inner)).astype(BF16)
        sv[...] += dot(prob.astype(BF16), grad)
        sk[...] += dot(grad_score, query)
        dq_ref[at, :] = (dot_tn(grad_score, key) * SCALING).astype(BF16)
        return carry

    sk[...] = jnp.zeros_like(sk)
    sv[...] = jnp.zeros_like(sv)
    lax.fori_loop(0, tokens // block, step, 0)
    dk_ref[...] = (sk[...] * SCALING).astype(BF16)
    dv_ref[...] = sv[...].astype(BF16)


def attend_back(query, key, value, grad, mixed, lse, first, heads):
    tokens, width = query.shape
    mine = pl.BlockSpec((tokens, HP), lambda h: (0, h + first))
    made = pl.BlockSpec((tokens, HP), lambda h: (0, h))
    width = heads * HP

    def attend_back_body(*refs):
        attend_back_kernel(*refs, first=first)

    return pl.pallas_call(
        attend_back_body,
        out_shape=[full((tokens, width), BF16)] * 3,
        grid=(heads,),
        in_specs=[mine] * 5 + [pl.BlockSpec(lse.shape, lambda h: (0, 0))],
        out_specs=[made] * 3,
        scratch_shapes=[pltpu.VMEM((tokens, HP), F32)] * 2,
        compiler_params=params(32),
        cost_estimate=cost(10 * tokens * tokens * width, 18 * tokens * width),
        name="attend_back",
    )(query, key, value, grad, mixed, lse)


def first_kernel(*refs):
    *parts, w_ref, lat_ref, term_ref, sum_ref, pack_ref = refs
    group = pack_ref.shape[1] // 3
    halves = len(parts) // 3
    for which in range(3):
        at = which * group
        for half in range(halves):
            ref = parts[half * 3 + which]
            for head in range(ref.shape[1] // HP):
                pack_ref[:, at : at + HD] = ref[:, head * HP : head * HP + HD]
                at += HD
    term = dot_nt(pack_ref[...], w_ref[...]).astype(BF16)
    term_ref[...] = term
    normal, _ = normalize(lat_ref[...].astype(F32))
    term = term.astype(F32)
    sum_ref[0:1, :] = total(term)
    sum_ref[1:2, :] = total(term * normal)


def first_term(parts, weight, latent, held, index, block):
    model, wide = weight.shape
    tokens = latent.shape[0]
    return call(
        first_kernel, index,
        [(v, block) for v in parts] + [(weight, None), (latent, block)],
        [
            (full((block, model), BF16), None, None),
            (full((8, model), F32), None, None),
            (full((tokens, wide), BF16), block, held),
        ],
        name="first_term", flops=2 * block * model * wide, size=2 * model * wide,
    )


def final_kernel(end_ref, near_ref, far_ref, lat_ref, gmid_ref, mod_ref, out_ref):
    grad = jnp.where(end_ref[0] == 1, far_ref[...].astype(F32), near_ref[...].astype(F32))
    normal, inverse = normalize(lat_ref[...].astype(F32))
    scale = 1.0 + mod_ref[SCALE_A : SCALE_A + 1, :]
    out_ref[...] = (gmid_ref[...] + normalize_back(normal, inverse, grad * scale)).astype(BF16)


def final(end, near, far, latent, grad_middle, mod, held, index, block):
    return call(
        final_kernel, index,
        [(near, None), (far, None), (latent, block), (grad_middle, block), (mod, None)],
        [(full(latent.shape, BF16), block, held)],
        scalars=(end,), name="final", mib=24, size=12 * block * latent.shape[1],
    )


def output_kernel(end_ref, near_ref, far_ref, tot_ref, lat_ref, cot_ref, mod_ref, bo_ref, b2_ref, sum_ref, out_ref):
    branch = jnp.where(end_ref[0] == 1, far_ref[...].astype(F32), near_ref[...].astype(F32))
    branch += b2_ref[...]
    attn = tot_ref[...].astype(F32) + bo_ref[...]
    middle = lat_ref[...].astype(F32) + mod_ref[GATE_A : GATE_A + 1, :] * attn
    out_ref[...] = (middle + mod_ref[GATE_M : GATE_M + 1, :] * branch).astype(BF16)
    sum_ref[0:1, :] = total(cot_ref[...].astype(F32) * branch)


def output_rows(end, near, far, tot, latent, cotangent, mod, b_out, b_fc2, held, index, block):
    model = latent.shape[1]
    return call(
        output_kernel, index,
        [
            (near, None), (far, None), (tot, block), (latent, block), (cotangent, block),
            (mod, None), (b_out, None), (b_fc2, None),
        ],
        [(full((8, model), F32), None, None), (full(latent.shape, BF16), block, held)],
        scalars=(end,), name="output", mib=24, size=12 * block * model,
    )


def add_kernel(a_ref, b_ref, o_ref):
    o_ref[...] = (a_ref[...].astype(F32) + b_ref[...].astype(F32)).astype(BF16)


def add(a, b):
    return pl.pallas_call(
        add_kernel,
        out_shape=jax.ShapeDtypeStruct(a.shape, BF16),
        compiler_params=params(8),
        cost_estimate=cost(a.size, 6 * a.size),
        name="add",
    )(a, b)


class Order:
    def __init__(self):
        self.last = None

    def __call__(self, step, *values):
        if self.last is not None:
            *values, _ = lax.optimization_barrier((*values, self.last))
        result = step(*values)
        self.last = result[0] if isinstance(result, (tuple, list)) else result
        return result


def build(groups, replicas):
    line = groups == 4

    def hop(value, pairs):
        return lax.ppermute(value, "mp", pairs)

    def gather_groups(value):
        if not line:
            return lax.all_gather(value, "mp", axis=0)
        rank = lax.axis_index("mp")
        turned = [value] + [hop(value, [(j, (j - d) % 4) for j in range(4)]) for d in (1, 2, 3)]
        turned = jnp.stack(turned + turned)
        return lax.dynamic_slice_in_dim(turned, (4 - rank) % 4, 4, 0)

    def local(
        latent, condition, lengths, w_ada, b_ada, w_qkv, b_qv, w_out, b_out,
        w_fc1, b_fc1, w_fc2, b_fc2, cotangent,
    ):
        tokens, model = latent.shape
        group = w_qkv.shape[2]
        heads = group // HD
        chunks = tokens // BLOCK_LANES
        block = BLOCK_LANES
        rank = lax.axis_index("mp")
        order = Order()
        part_width = w_ada.shape[1]

        mod_part = modulate(condition, w_ada, b_ada)
        modulation = gather_groups(mod_part).reshape(6, model)
        mod = jnp.pad(modulation, ((0, 2), (0, 0)))
        end = ((rank == 0) | (rank == groups - 1)).astype(jnp.int32).reshape(1)
        if not line:
            end = jnp.zeros((1,), jnp.int32)

        qkv_weight = w_qkv.reshape(model, 3 * group)
        qv_bias = b_qv.astype(F32)
        qkv_bias = jnp.concatenate([qv_bias[0], jnp.zeros((group,), F32), qv_bias[1]]).reshape(1, -1)
        out_bias = b_out.astype(F32).reshape(1, model)
        fc1_bias = b_fc1.astype(F32).reshape(1, -1)
        fc2_bias = b_fc2.astype(F32).reshape(1, model)

        normed_one, query, key, value = project(lengths, latent, mod, qkv_weight, qkv_bias, block)
        order.last = normed_one

        terms, first, mid, near, far = {}, {}, {}, {}, {}

        def send(job, term):
            terms[job] = term
            if line:
                first[job] = hop(term, IN_HOP)
            else:
                near[job] = far[job] = lax.psum(term, "mp")

        def relay(job):
            if line:
                mid[job] = order(add, terms[job], first[job])
                first[job] = hop(mid[job], MID_HOP)

        def spread_out(job):
            if line:
                near[job] = order(add, mid[job], first[job])
                far[job] = hop(near[job], OUT_HOP)

        state = {
            "att": (None,) * 3, "feed": (None,) * 5, "mid": (None,) * 3, "first": None,
            "final": None, "out": None, "hidden": [], "middle": [], "ends": [], "gate": [],
        }

        def do_attend(k):
            term, *state["att"] = order(
                lambda q, *held: attend(q, key, value, w_out, held or (None,) * 3, k, block),
                query, *[v for v in state["att"] if v is not None],
            )
            send(("a", k), term)

        def do_feed(k):
            term, sums, *state["feed"] = order(
                lambda a, b, *held: feed(
                    end, a, b, latent, cotangent, mod, out_bias, w_fc1, fc1_bias, w_fc2,
                    held or (None,) * 5, k, block,
                ),
                near["a", k], far["a", k], *[v for v in state["feed"] if v is not None],
            )
            state["hidden"].append(sums[0:1])
            send(("g", k), term)

        def do_middle(k):
            sums, *state["mid"] = order(
                lambda a, b, *held: middle_back(
                    end, a, b, state["feed"][0], latent, cotangent, mod, out_bias, w_out,
                    held or (None,) * 3, k, block,
                ),
                near["g", k], far["g", k], *[v for v in state["mid"] if v is not None],
            )
            state["middle"].append(sums)

        def do_back(start, count):
            return order(
                lambda g: attend_back(query, key, value, g, *state["att"][1:], start, count),
                state["mid"][2],
            )

        def do_first(k, parts):
            term, sums, state["first"] = order(
                lambda q, *held: first_term(
                    [q, *parts[1:]], qkv_weight, latent, held[0] if held else None, k, block
                ),
                parts[0], *([] if state["first"] is None else [state["first"]]),
            )
            state["ends"].append(sums)
            send(("f", k), term)

        def do_final(k):
            (state["final"],) = order(
                lambda a, b, *held: final(
                    end, a, b, latent, state["mid"][1], mod, held[0] if held else None, k, block
                ),
                near["f", k], far["f", k], *([] if state["final"] is None else [state["final"]]),
            )

        def do_output(k):
            sums, state["out"] = order(
                lambda a, b, *held: output_rows(
                    end, a, b, state["feed"][0], latent, cotangent, mod, out_bias, fc2_bias,
                    held[0] if held else None, k, tokens // 2,
                ),
                near["m", k], far["m", k], *([] if state["out"] is None else [state["out"]]),
            )
            state["gate"].append(sums[0:1])

        def cast_dot(a, b):
            return dot_tn(a, b).astype(BF16)

        for k in range(chunks):
            do_attend(k)
        relay(("a", 0))
        relay(("a", 1))
        spread_out(("a", 0))
        relay(("a", 2))
        spread_out(("a", 1))
        do_feed(0)
        relay(("a", 3))
        spread_out(("a", 2))
        do_feed(1)
        spread_out(("a", 3))
        do_feed(2)
        relay(("g", 0))
        do_feed(3)
        attn_sum, normed_two, act, grad_hidden, grad_mlp = state["feed"]
        half = tokens // 2
        mlp = order(lambda a: dot(a, w_fc2).astype(BF16), act)
        relay(("g", 1))
        spread_out(("g", 0))
        send(("m", 0), mlp[:half])
        send(("m", 1), mlp[half:])
        grad_fc2 = order(cast_dot, act, grad_mlp)
        relay(("g", 2))
        spread_out(("g", 1))
        do_middle(0)
        grad_fc1 = order(cast_dot, normed_two, grad_hidden)
        grad_fc1, grad_fc2 = lax.psum((grad_fc1, grad_fc2), "dp")
        relay(("g", 3))
        spread_out(("g", 2))
        do_middle(1)
        spread_out(("g", 3))
        do_middle(2)
        do_middle(3)
        some = max(heads // 2, 1)
        parts = [*do_back(0, some)]
        relay(("m", 0))
        if heads > some:
            parts += do_back(some, heads - some)
        for k in range(chunks):
            do_first(k, parts)
        relay(("m", 1))
        spread_out(("m", 0))
        grad_out_proj = order(cast_dot, state["att"][0], state["mid"][0])
        grad_qkv = order(cast_dot, normed_one, state["first"])
        end_sums = sum(state["ends"])[0:2]
        end_parts = gather_groups(end_sums)
        relay(("f", 0))
        spread_out(("m", 1))
        do_output(0)
        relay(("f", 1))
        spread_out(("f", 0))
        do_output(1)
        output = state["out"]

        end_sums = jnp.sum(end_parts, axis=0)
        mid_sums = sum(state["middle"])
        grad_modulation = jnp.concatenate(
            [end_sums, mid_sums[2:3], mid_sums[0:2], sum(state["gate"])], axis=0
        ).reshape(1, 6 * model)
        mod_grad = lax.dynamic_slice_in_dim(grad_modulation, rank * part_width, part_width, 1)
        cond_parts = gather_groups(order(condition_term, mod_grad, w_ada))
        packed = state["first"].astype(F32)
        cond = condition.astype(F32)
        small = [
            jax.nn.silu(cond), mod_grad, sum(state["hidden"]), total(grad_mlp.astype(F32)),
            mid_sums[3:4], total(packed[:, :group]), total(packed[:, 2 * group :]),
        ]
        gathered = order(
            lambda v: lax.all_gather(v, "dp", axis=0, tiled=True), jnp.concatenate(small, axis=1)
        )
        cuts = [0]
        for v in small:
            cuts.append(cuts[-1] + v.shape[1])
        pieces = [gathered[:, a:b] for a, b in zip(cuts[:-1], cuts[1:])]
        relay(("f", 2))
        spread_out(("f", 1))
        do_final(0)
        grad_ada = order(outer, *pieces[:2])
        relay(("f", 3))
        spread_out(("f", 2))
        do_final(1)
        spread_out(("f", 3))
        do_final(2)
        grad_silu = jnp.sum(cond_parts, axis=0)
        _, silu_back = jax.vjp(jax.nn.silu, cond)
        grad_condition = silu_back(grad_silu)[0]
        grad_qkv, grad_out_proj, *_ = lax.optimization_barrier(
            (grad_qkv, grad_out_proj, grad_fc1, grad_fc2)
        )
        grad_qkv, grad_out_proj = lax.psum((grad_qkv, grad_out_proj), "dp")
        do_final(3)
        sums = [jnp.sum(v, axis=0) for v in pieces[1:]]
        return (
            output,
            state["final"],
            grad_condition,
            grad_ada,
            sums[0],
            grad_qkv.astype(F32).reshape(model, 3, group),
            jnp.stack([sums[4], sums[5]]),
            grad_out_proj.astype(F32),
            sums[3],
            grad_fc1.astype(F32),
            sums[1],
            grad_fc2.astype(F32),
            sums[2],
        )

    return local


def solution(mesh):
    rows, cols, last = P("dp", None), P(None, "mp"), P("mp")
    deep = P(None, None, "mp")
    tall = P("mp", None)
    return jax.shard_map(
        build(mesh.shape["mp"], mesh.shape["dp"]),
        mesh=mesh,
        in_specs=(
            rows, rows, P("dp"), cols, last, deep, cols, tall, P(), cols, last, tall, P(), rows,
        ),
        out_specs=(rows, rows, rows, cols, last, deep, cols, tall, P(), cols, last, tall, P()),
        check_vma=False,
    )
```
